32 devices in a mesh: band: 4 (over x, core), gx: 4 (over z), gy: 2 (over y).
Axes of the slice: x: 2, y: 2, z: 4, core: 2. Of those that a mesh axis runs over, the one named last changes fastest.
Arguments:
- local_orbitals: float32 [4, 32, 32, 128], P('band', 'gx', 'gy'), may hold values from -14 to 14
- block_orbitals: float32 [24, 8, 32, 32, 128], P('band', None, 'gx', 'gy'), may hold values from -14 to 14
- occupation: float32 [24, 8], replicated, may hold values from 0.2 to 2
- owner: int32 [4], replicated, may hold values from 0 to 3
- block_id: int32 [4], replicated, may hold values from 0 to 5
Outputs:
- exchange: float32 [4, 32, 32, 128], P('band', 'gx', 'gy')
The draws below stay inside these ranges and needn't reach their ends.
All inputs are finite; a program needn't handle non-finite values.
Results may differ from the reference program's by a relative error of at most 0.0001.
Values sent between devices are 32-bit elements; how exact they have to be, the bound alone decides.
A program may use at most 64 MiB of HBM per device.

```python
import math
import jax
import jax.numpy as jnp
from jax import lax

NZ = 128
BLOCK = 8
BLOCKS_DEV = 6
TURNS = 4
ITERS = 4
NX = 32
NY = 32
NLOC = 4
BLOCKS = 24
N_BAND = 4


def orbital_values(key, shape):
    noise_key, scale_key = jax.random.split(key)
    rank = len(shape)
    grid_first = lax.broadcasted_iota(jnp.float32, shape, rank - 3) / NX
    spread = jnp.exp(math.log(10.0) * (jax.random.uniform(scale_key, shape, jnp.float32) - 1.0))
    noise = jnp.clip(jax.random.normal(noise_key, shape, jnp.float32), -4.0, 4.0)
    ramp_along = jnp.exp(0.5 * math.log(3.0) * grid_first)
    return 2.0 * noise * spread * ramp_along


def draw_local_orbitals(key, part):
    return orbital_values(jax.random.fold_in(key, 11), (NLOC, NX, NY, NZ))


def draw_block_orbitals(key, part):
    return orbital_values(jax.random.fold_in(key, 23), (BLOCKS, BLOCK, NX, NY, NZ))


def place_ends(entries, rng, low, high):
    dims = entries.shape
    place = [jax.random.randint(jax.random.fold_in(rng, axis), (), 0, dims[axis]) for axis in range(len(dims))]
    entries = entries.at[tuple(place)].set(low)
    longest = dims.index(max(dims))
    place[longest] = (place[longest] + 1) % dims[longest]
    return entries.at[tuple(place)].set(high)


def setup_inputs(seed: int = 0) -> dict:
    key_list = jax.random.split(jax.random.key(seed), 6)
    local_orbitals = draw_local_orbitals(jax.random.fold_in(key_list[5], 71), 0)
    block_orbitals = draw_block_orbitals(jax.random.fold_in(key_list[5], 71), 0)
    occupation = jnp.clip(jax.random.uniform(key_list[2], (BLOCKS, BLOCK), jnp.float32, 0.2, 2.0), 0.2, 2.0)
    owner = place_ends(jax.random.randint(key_list[3], (TURNS,), 0, N_BAND), jax.random.fold_in(key_list[3], 1), 0, N_BAND - 1).astype(jnp.int32)
    block_id = place_ends(jax.random.randint(key_list[4], (TURNS,), 0, BLOCKS_DEV), jax.random.fold_in(key_list[4], 1), 0, BLOCKS_DEV - 1).astype(jnp.int32)
    return dict(local_orbitals=local_orbitals, block_orbitals=block_orbitals, occupation=occupation, owner=owner, block_id=block_id)


SCREEN = 0.1


def operate(field_in):
    beside = jnp.roll(field_in, 1, axis=1) + jnp.roll(field_in, -1, axis=1)
    beside = beside + jnp.roll(field_in, 1, axis=2) + jnp.roll(field_in, -1, axis=2)
    beside = beside + jnp.roll(field_in, 1, axis=3) + jnp.roll(field_in, -1, axis=3)
    return (6.0 + SCREEN) * field_in - beside


def per_field(values):
    return values[:, None, None, None]


def solve_pairs(density):
    solution = jnp.zeros_like(density)
    residual = density
    direction = density
    norm_now = jnp.sum(residual * residual, axis=(1, 2, 3))
    for iteration in range(ITERS):
        image = operate(direction)
        step_length = norm_now / jnp.sum(direction * image, axis=(1, 2, 3))
        solution = solution + per_field(step_length) * direction
        residual = residual - per_field(step_length) * image
        norm_next = jnp.sum(residual * residual, axis=(1, 2, 3))
        direction = residual + per_field(norm_next / norm_now) * direction
        norm_now = norm_next
    return solution


def reference(local_orbitals, block_orbitals, occupation, owner, block_id):
    result = jnp.zeros(local_orbitals.shape, jnp.float32)
    for turn_index in range(TURNS):
        global_pick = (owner[turn_index] * BLOCKS_DEV + block_id[turn_index]).astype(jnp.int32)
        fields = lax.dynamic_index_in_dim(block_orbitals, global_pick, 0, keepdims=False)
        weights = lax.dynamic_index_in_dim(occupation, global_pick, 0, keepdims=False)
        weighted = per_field(weights) * fields

        def one_orbital(orbital):
            solution = solve_pairs(orbital[None] * fields)
            return jnp.sum(solution * weighted, axis=0)

        result = result - lax.map(one_orbital, local_orbitals)
    return result
```

```python
import functools
import math

import jax
import jax.numpy as jnp
from jax import lax
from jax.experimental import pallas as pl
from jax.experimental.pallas import tpu as pltpu
from jax.sharding import PartitionSpec as P

SCREEN = 0.1
DIAGONAL = 6.0 + SCREEN
HALO = 4
NOISE = 1e-6


def apply_row(read, x, ny):
    centre = read(x, 1, ny - 1)
    beside = read(x - 1, 1, ny - 1) + read(x + 1, 1, ny - 1)
    beside = beside + read(x, 0, ny - 2) + read(x, 2, ny)
    lanes = centre.shape[-1]
    beside = beside + pltpu.roll(centre, 1, 2) + pltpu.roll(centre, lanes - 1, 2)
    return DIAGONAL * centre - beside


def cg_kernel(
    n_gx, n_gy, fields_ref, orb_ref, weight_ref, out_ref,
    dens, v1, v2, d2, w, coef, part, parts, send_sem, recv_sem,
):
    ex, ey, nf, nz = fields_ref.shape
    nl = orb_ref.shape[0]
    nx, ny = ex - 2 * HALO, ey - 2 * HALO
    group = n_gx * n_gy
    gx, gy = lax.axis_index("gx"), lax.axis_index("gy")
    me = gx * n_gy + gy
    lane = lax.broadcasted_iota(jnp.int32, (nf, nz), 1)

    def device(index):
        return {"gx": index // n_gy, "gy": lax.rem(index, n_gy)}

    barrier = pltpu.get_barrier_semaphore()

    def greet(off, c):
        pl.semaphore_signal(
            barrier, inc=1, device_id=device(lax.rem(me + off, group)),
            device_id_type=pl.DeviceIdType.MESH,
        )
        return c

    lax.fori_loop(1, group, greet, 0)

    def pack(sums):
        total = jnp.zeros((nf, nz), jnp.float32)
        for m, acc in enumerate(sums):
            value = jnp.sum(acc, axis=1, keepdims=True)
            total = jnp.where(lane == m, jnp.broadcast_to(value, (nf, nz)), total)
        return total

    def unpack(total, m):
        value = jnp.sum(jnp.where(lane == m, total, 0.0), axis=1, keepdims=True)
        return jnp.broadcast_to(value, (nf, nz))

    def copy_to(r, index):
        return pltpu.make_async_remote_copy(
            src_ref=part.at[r], dst_ref=parts.at[r, me],
            send_sem=send_sem.at[r, index], recv_sem=recv_sem.at[r, me],
            device_id=device(index), device_id_type=pl.DeviceIdType.MESH,
        )

    def arrival(r, index):
        return pltpu.make_async_remote_copy(
            src_ref=part.at[r], dst_ref=parts.at[r, index],
            send_sem=send_sem.at[r, index], recv_sem=recv_sem.at[r, index],
            device_id=device(index), device_id_type=pl.DeviceIdType.MESH,
        )

    def all_reduce(r):
        def start(off, c):
            copy_to(r, lax.rem(me + off, group)).start()
            return c

        def finish(off, c):
            index = lax.rem(me + off, group)
            arrival(r, index).wait_recv()
            copy_to(r, index).wait_send()
            return c

        lax.fori_loop(1, group, start, 0)
        parts[r, me] = part[r]
        lax.fori_loop(1, group, finish, 0)
        return lax.fori_loop(1, group, lambda s, t: t + parts[r, s], parts[r, 0])

    def density(i, x, lo, hi):
        return fields_ref[x, lo:hi] * orb_ref[i, x, lo:hi][:, None, :]

    def inner(sums, pairs):
        return tuple(s + jnp.sum(a * b, axis=0) for s, (a, b) in zip(sums, pairs))

    zero = jnp.zeros((nf, nz), jnp.float32)

    def basis(i, c):
        def row0(x, c):
            dens[x] = density(i, x, 0, ey)
            return c

        def row1(x, c):
            v1[i, x] = apply_row(lambda p, lo, hi: dens[p, lo:hi], x + 1, ey)
            return c

        def row2(x, c):
            v2[i, x] = apply_row(lambda p, lo, hi: v1[i, p, lo:hi], x + 1, ey - 2)
            return c

        def products(x, sums):
            b = dens[x + 4, 4 : 4 + ny]
            a1 = v1[i, x + 3, 3 : 3 + ny]
            a2 = v2[i, x + 2, 2 : 2 + ny]
            return inner(sums, ((b, b), (b, a1), (a1, a1), (a1, a2), (a2, a2)))

        lax.fori_loop(0, ex, row0, 0)
        lax.fori_loop(0, ex - 2, row1, 0)
        lax.fori_loop(0, ex - 4, row2, 0)
        part[0, i] = pack(lax.fori_loop(0, nx, products, (zero,) * 5))
        return c

    lax.fori_loop(0, nl, basis, 0)
    pl.semaphore_wait(barrier, group - 1)
    total = all_reduce(0)
    for i in range(nl):
        m0, m1, m2, m3, m4 = (unpack(total[i], m) for m in range(5))
        s0 = m0 / m1
        rr1 = s0 * s0 * m2 - 2.0 * s0 * m1 + m0
        small = rr1 <= NOISE * m0
        b0 = rr1 / m0
        g = 1.0 + b0
        curve = g * g * m1 - 2.0 * g * s0 * m2 + s0 * s0 * m3
        s1 = jnp.where(small, 0.0, rr1 / jnp.where(small, 1.0, curve))
        image2 = g * g * m2 - 2.0 * g * s0 * m3 + s0 * s0 * m4
        rr2 = jnp.maximum(s1 * s1 * image2 - rr1, 0.0)
        b1 = jnp.where(small, 0.0, rr2 / jnp.where(small, 1.0, rr1))
        coef[i, 0], coef[i, 1], coef[i, 2], coef[i, 3] = s0, g, s1, b1

    def second(i, c):
        s0, g, s1, b1 = coef[i, 0], coef[i, 1], coef[i, 2], coef[i, 3]
        cb = 1.0 + b1 * g
        c1 = -(s0 + s1 * g) - b1 * s0
        c2 = s1 * s0

        def row_d(x, c):
            b = density(i, x + 2, 2, ey - 2)
            d2[i, x] = cb * b + c1 * v1[i, x + 1, 1 : ey - 3] + c2 * v2[i, x]
            return c

        def row_w(x, c):
            w[i, x] = apply_row(lambda p, lo, hi: d2[i, p, lo:hi], x + 1, ey - 4)
            return c

        def products(x, sums):
            b = density(i, x + 4, 4, 4 + ny)
            a1 = v1[i, x + 3, 3 : 3 + ny]
            a2 = v2[i, x + 2, 2 : 2 + ny]
            dd = d2[i, x + 2, 2 : 2 + ny]
            ww = w[i, x + 1, 1 : 1 + ny]
            r2 = dd - b1 * (g * b - s0 * a1)
            ad1 = g * a1 - s0 * a2
            aw = apply_row(lambda p, lo, hi: w[i, p, lo:hi], x + 1, ey - 6)
            return inner(
                sums,
                ((r2, r2), (r2, ww), (dd, ww), (ww, ww), (r2, ad1), (ww, ad1), (ww, aw)),
            )

        lax.fori_loop(0, ex - 4, row_d, 0)
        lax.fori_loop(0, ex - 6, row_w, 0)
        part[1, i] = pack(lax.fori_loop(0, nx, products, (zero,) * 7))
        return c

    lax.fori_loop(0, nl, second, 0)
    total = all_reduce(1)
    for i in range(nl):
        rr, rw, dw, ww, ra, wa, waw = (unpack(total[i], m) for m in range(7))
        b1 = coef[i, 3]
        s2 = rr / dw
        rr3 = rr - 2.0 * s2 * rw + s2 * s2 * ww
        small = rr3 <= NOISE * rr
        b2 = rr3 / rr
        r_ar = rw - b1 * ra
        w_ar = ww - b1 * wa
        curve = r_ar + s2 * s2 * waw + b2 * b2 * dw
        curve = curve - 2.0 * s2 * w_ar + 2.0 * b2 * rw - 2.0 * s2 * b2 * ww
        s3 = jnp.where(small, 0.0, rr3 / jnp.where(small, 1.0, curve))
        coef[i, 4], coef[i, 5], coef[i, 6] = s2, b2, s3

    weight = weight_ref[...]

    def combine(i, c):
        s0, g, s1, b1 = coef[i, 0], coef[i, 1], coef[i, 2], coef[i, 3]
        s2, b2, s3 = coef[i, 4], coef[i, 5], coef[i, 6]
        k1 = s1 - s3 * b1
        cb, c1 = s0 + k1 * g, -k1 * s0
        cd, cw = s2 + s3 * (1.0 + b2), -s3 * s2
        cb, c1, cd, cw = cb * weight, c1 * weight, cd * weight, cw * weight

        def row(x, c):
            f = fields_ref[x + 4, 4 : 4 + ny]
            b = f * orb_ref[i, x + 4, 4 : 4 + ny][:, None, :]
            sol = cb * b + c1 * v1[i, x + 3, 3 : 3 + ny]
            sol = sol + cd * d2[i, x + 2, 2 : 2 + ny] + cw * w[i, x + 1, 1 : 1 + ny]
            out_ref[i, x] = -jnp.sum(sol * f, axis=1)
            return c

        lax.fori_loop(0, nx, row, 0)
        return c

    lax.fori_loop(0, nl, combine, 0)


def run_cg(mesh, fields, orbitals, weight):
    n_gx, n_gy = mesh.shape["gx"], mesh.shape["gy"]
    group = n_gx * n_gy
    ex, ey, nf, nz = fields.shape
    nl = orbitals.shape[0]
    vmem = pl.BlockSpec(memory_space=pltpu.VMEM)
    f32 = jnp.float32
    return pl.pallas_call(
        functools.partial(cg_kernel, n_gx, n_gy),
        out_shape=jax.ShapeDtypeStruct((nl, ex - 2 * HALO, ey - 2 * HALO, nz), f32),
        in_specs=[vmem] * 3,
        out_specs=vmem,
        scratch_shapes=[
            pltpu.VMEM((ex, ey, nf, nz), f32),
            pltpu.VMEM((nl, ex - 2, ey - 2, nf, nz), f32),
            pltpu.VMEM((nl, ex - 4, ey - 4, nf, nz), f32),
            pltpu.VMEM((nl, ex - 4, ey - 4, nf, nz), f32),
            pltpu.VMEM((nl, ex - 6, ey - 6, nf, nz), f32),
            pltpu.VMEM((nl, 7, nf, nz), f32),
            pltpu.VMEM((2, nl, nf, nz), f32),
            pltpu.VMEM((2, group, nl, nf, nz), f32),
            pltpu.SemaphoreType.DMA((2, group)),
            pltpu.SemaphoreType.DMA((2, group)),
        ],
        compiler_params=pltpu.CompilerParams(
            collective_id=0, has_side_effects=True, vmem_limit_bytes=48 << 20
        ),
    )(fields, orbitals, weight)


def extend(arrays, axis, dim):
    count = lax.axis_size(axis)
    forward = [(i, (i + 1) % count) for i in range(count)]
    backward = [(target, source) for source, target in forward]
    nz = arrays[0].shape[-1]

    def travel(slabs, pairs):
        flat = jnp.concatenate([s.reshape(-1, nz) for s in slabs])
        flat = lax.ppermute(flat, axis, pairs)
        sizes = [math.prod(s.shape[:-1]) for s in slabs]
        ends = [sum(sizes[: i + 1]) for i in range(len(sizes))]
        return [
            flat[end - size : end].reshape(s.shape)
            for s, size, end in zip(slabs, sizes, ends)
        ]

    lows = travel([lax.slice_in_dim(a, a.shape[dim] - HALO, None, axis=dim) for a in arrays], forward)
    highs = travel([lax.slice_in_dim(a, 0, HALO, axis=dim) for a in arrays], backward)
    return [jnp.concatenate([l, a, h], axis=dim) for l, a, h in zip(lows, arrays, highs)]


def on_device(mesh, local_orbitals, block_orbitals, occupation, owner, block_id):
    n_band = mesh.shape["band"]
    band = lax.axis_index("band")
    turns = owner.shape[0]
    blocks_dev, block = block_orbitals.shape[:2]
    share = block // n_band
    picked = block_orbitals[block_id]
    mine = (owner == band)[:, None, None, None, None]
    picked = jnp.where(mine, picked, 0.0)
    fields = lax.psum_scatter(picked, "band", scatter_dimension=1, tiled=True)
    weights = occupation[owner * blocks_dev + block_id]
    weights = lax.dynamic_slice_in_dim(weights, band * share, share, axis=1)
    fields = fields.reshape((turns * share,) + fields.shape[2:])
    fields = jnp.transpose(fields, (1, 2, 0, 3))
    arrays = extend([fields, local_orbitals[0]], "gx", 0)
    fields, orbital = extend(arrays, "gy", 1)
    orbitals = lax.all_gather(orbital, "band")
    weight = jnp.broadcast_to(weights.reshape(-1, 1), fields.shape[2:])
    result = run_cg(mesh, fields, orbitals, weight)
    return lax.psum_scatter(result, "band", scatter_dimension=0, tiled=True)


def solution(mesh):
    placed = (P("band", "gx", "gy", None), P("band", None, "gx", "gy", None), P(), P(), P())
    return jax.shard_map(
        functools.partial(on_device, mesh),
        mesh=mesh,
        in_specs=placed,
        out_specs=P("band", "gx", "gy", None),
        check_vma=False,
    )
```

```python
import functools

import jax
import jax.numpy as jnp
from jax import lax
from jax.experimental import pallas as pl
from jax.experimental.pallas import tpu as pltpu
from jax.sharding import PartitionSpec as P

SCREEN = 0.1
DIAGONAL = 6.0 + SCREEN
HALO = 4
CORES = 2
NOISE = 1e-6


def apply_row(read, x, ny):
    centre = read(x, 1, ny - 1)
    beside = read(x - 1, 1, ny - 1) + read(x + 1, 1, ny - 1)
    beside = beside + read(x, 0, ny - 2) + read(x, 2, ny)
    lanes = centre.shape[-1]
    beside = beside + pltpu.roll(centre, 1, 2) + pltpu.roll(centre, lanes - 1, 2)
    return DIAGONAL * centre - beside


def cg_kernel(
    n_band, n_gx, n_gy, owner_ref, picked_ref, local_ref, weight_ref, out_ref,
    fields_ref, orb_ref, from_mate, combined, from_far, results, results_in,
    dens, v1, v2, d2, w, coef, part, parts, send_sem, recv_sem,
    mate_sem, far_sem, orb_sem, halo_sem, result_sem,
):
    ex, ey, nf, nz = fields_ref.shape
    nl = orb_ref.shape[0]
    turns, n_chip, cores, share = picked_ref.shape[:4]
    per_band = nl // n_band
    nx, ny = ex - 2 * HALO, ey - 2 * HALO
    group = n_gx * n_gy
    band, gx, gy = (lax.axis_index(axis) for axis in ("band", "gx", "gy"))
    me = gx * n_gy + gy
    chip, core = band // cores, lax.rem(band, cores)
    mate = chip * cores + 1 - core
    lane = lax.broadcasted_iota(jnp.int32, (nf, nz), 1)
    inside_x, inside_y = pl.ds(HALO, nx), pl.ds(HALO, ny)

    def device(index):
        return {"gx": index // n_gy, "gy": lax.rem(index, n_gy)}

    def remote(src, dst, sems, target):
        return pltpu.make_async_remote_copy(
            src_ref=src, dst_ref=dst, send_sem=sems[0], recv_sem=sems[1],
            device_id=target, device_id_type=pl.DeviceIdType.MESH,
        )

    barrier = pltpu.get_barrier_semaphore()

    def greet(off, c):
        pl.semaphore_signal(
            barrier, inc=1, device_id=device(lax.rem(me + off, group)),
            device_id_type=pl.DeviceIdType.MESH,
        )
        return c

    def greet_band(off, c):
        pl.semaphore_signal(
            barrier, inc=1, device_id={"band": lax.rem(band + off, n_band)},
            device_id_type=pl.DeviceIdType.MESH,
        )
        return c

    lax.fori_loop(1, group, greet, 0)
    lax.fori_loop(1, n_band, greet_band, 0)
    pl.semaphore_wait(barrier, group + n_band - 2)

    to_mate = [
        remote(
            picked_ref.at[t, :, 1 - core], from_mate.at[t],
            (mate_sem.at[0, t], mate_sem.at[1, t]), {"band": mate},
        )
        for t in range(turns)
    ]
    for copy in to_mate:
        copy.start()
    orb_copies = [
        remote(
            local_ref, orb_ref.at[pl.ds(band * per_band, per_band), inside_x, inside_y],
            (orb_sem.at[0, off], orb_sem.at[1, off]), {"band": lax.rem(band + off, n_band)},
        )
        for off in range(1, n_band)
    ]
    for copy in orb_copies:
        copy.start()
    orb_ref[pl.ds(band * per_band, per_band), inside_x, inside_y] = local_ref[...]
    far = []
    for t in range(turns):
        to_mate[t].wait()
        by_mate = owner_ref[t] == mate
        for off in range(1, n_chip):
            there = lax.rem(chip + off, n_chip)
            combined[off - 1, t] = jnp.where(
                by_mate, from_mate[t, there], picked_ref[t, there, core]
            )
            copy = remote(
                combined.at[off - 1, t], from_far.at[off - 1, t],
                (far_sem.at[0, off - 1, t], far_sem.at[1, off - 1, t]),
                {"band": there * cores + core},
            )
            copy.start()
            far.append((t, copy))

    def halo(ref, lead, which):
        def along_x(lo, n, dst, target, k):
            src = ref.at[lead + (pl.ds(lo, n), inside_y)]
            dst = ref.at[lead + (pl.ds(dst, n), inside_y)]
            return remote(src, dst, (halo_sem.at[0, which, k], halo_sem.at[1, which, k]), target)

        def along_y(lo, n, dst, target, k):
            src = ref.at[lead + (slice(None), pl.ds(lo, n))]
            dst = ref.at[lead + (slice(None), pl.ds(dst, n))]
            return remote(src, dst, (halo_sem.at[0, which, k], halo_sem.at[1, which, k]), target)

        up, down = {"gx": lax.rem(gx + 1, n_gx)}, {"gx": lax.rem(gx + n_gx - 1, n_gx)}
        right, left = {"gy": lax.rem(gy + 1, n_gy)}, {"gy": lax.rem(gy + n_gy - 1, n_gy)}
        return (
            [along_x(nx, HALO, 0, up, 0), along_x(HALO, HALO, HALO + nx, down, 1)],
            [along_y(ny, HALO, 0, right, 2), along_y(HALO, HALO, HALO + ny, left, 3)],
        )

    for copy in orb_copies:
        copy.wait()
    orb_x, orb_y = halo(orb_ref, (slice(None),), 0)
    field_x, field_y = halo(fields_ref, (), 1)
    for copy in orb_x:
        copy.start()
    for copy in orb_x:
        copy.wait()
    for copy in orb_y:
        copy.start()
    for t in range(turns):
        for turn, copy in far:
            if turn == t:
                copy.wait()
        who = owner_ref[t]
        value = jnp.where(who == mate, from_mate[t, chip], picked_ref[t, chip, core])
        for off in range(1, n_chip):
            there = lax.rem(chip + n_chip - off, n_chip)
            value = jnp.where(who // cores == there, from_far[off - 1, t], value)
        for s in range(share):
            fields_ref[inside_x, inside_y, t * share + s, :] = value[s]
    for copies in (field_x, field_y):
        for copy in copies:
            copy.start()
        for copy in copies:
            copy.wait()
    for copy in orb_y:
        copy.wait()

    def pack(sums):
        total = jnp.zeros((nf, nz), jnp.float32)
        for m, acc in enumerate(sums):
            value = jnp.sum(acc, axis=1, keepdims=True)
            total = jnp.where(lane == m, jnp.broadcast_to(value, (nf, nz)), total)
        return total

    def unpack(total, m):
        value = jnp.sum(jnp.where(lane == m, total, 0.0), axis=1, keepdims=True)
        return jnp.broadcast_to(value, (nf, nz))

    def copy_to(r, index):
        return pltpu.make_async_remote_copy(
            src_ref=part.at[r], dst_ref=parts.at[r, me],
            send_sem=send_sem.at[r, index], recv_sem=recv_sem.at[r, me],
            device_id=device(index), device_id_type=pl.DeviceIdType.MESH,
        )

    def arrival(r, index):
        return pltpu.make_async_remote_copy(
            src_ref=part.at[r], dst_ref=parts.at[r, index],
            send_sem=send_sem.at[r, index], recv_sem=recv_sem.at[r, index],
            device_id=device(index), device_id_type=pl.DeviceIdType.MESH,
        )

    def all_reduce(r):
        def start(off, c):
            copy_to(r, lax.rem(me + off, group)).start()
            return c

        def finish(off, c):
            index = lax.rem(me + off, group)
            arrival(r, index).wait_recv()
            copy_to(r, index).wait_send()
            return c

        lax.fori_loop(1, group, start, 0)
        parts[r, me] = part[r]
        lax.fori_loop(1, group, finish, 0)
        return lax.fori_loop(1, group, lambda s, t: t + parts[r, s], parts[r, 0])

    def density(i, x, lo, hi):
        return fields_ref[x, lo:hi] * orb_ref[i, x, lo:hi]

    def inner(sums, pairs):
        return tuple(s + jnp.sum(a * b, axis=0) for s, (a, b) in zip(sums, pairs))

    zero = jnp.zeros((nf, nz), jnp.float32)

    def basis(i, c):
        def row0(x, c):
            dens[x] = density(i, x, 0, ey)
            return c

        def row1(x, c):
            v1[i, x] = apply_row(lambda p, lo, hi: dens[p, lo:hi], x + 1, ey)
            return c

        def row2(x, c):
            v2[i, x] = apply_row(lambda p, lo, hi: v1[i, p, lo:hi], x + 1, ey - 2)
            return c

        def products(x, sums):
            b = dens[x + 4, 4 : 4 + ny]
            a1 = v1[i, x + 3, 3 : 3 + ny]
            a2 = v2[i, x + 2, 2 : 2 + ny]
            return inner(sums, ((b, b), (b, a1), (a1, a1), (a1, a2), (a2, a2)))

        lax.fori_loop(0, ex, row0, 0)
        lax.fori_loop(0, ex - 2, row1, 0)
        lax.fori_loop(0, ex - 4, row2, 0)
        part[0, i] = pack(lax.fori_loop(0, nx, products, (zero,) * 5))
        return c

    lax.fori_loop(0, nl, basis, 0)
    total = all_reduce(0)
    for i in range(nl):
        m0, m1, m2, m3, m4 = (unpack(total[i], m) for m in range(5))
        s0 = m0 / m1
        rr1 = s0 * s0 * m2 - 2.0 * s0 * m1 + m0
        small = rr1 <= NOISE * m0
        b0 = rr1 / m0
        g = 1.0 + b0
        curve = g * g * m1 - 2.0 * g * s0 * m2 + s0 * s0 * m3
        s1 = jnp.where(small, 0.0, rr1 / jnp.where(small, 1.0, curve))
        image2 = g * g * m2 - 2.0 * g * s0 * m3 + s0 * s0 * m4
        rr2 = jnp.maximum(s1 * s1 * image2 - rr1, 0.0)
        b1 = jnp.where(small, 0.0, rr2 / jnp.where(small, 1.0, rr1))
        coef[i, 0], coef[i, 1], coef[i, 2], coef[i, 3] = s0, g, s1, b1

    def second(i, c):
        s0, g, s1, b1 = coef[i, 0], coef[i, 1], coef[i, 2], coef[i, 3]
        cb = 1.0 + b1 * g
        c1 = -(s0 + s1 * g) - b1 * s0
        c2 = s1 * s0

        def row_d(x, c):
            b = density(i, x + 2, 2, ey - 2)
            d2[i, x] = cb * b + c1 * v1[i, x + 1, 1 : ey - 3] + c2 * v2[i, x]
            return c

        def row_w(x, c):
            w[i, x] = apply_row(lambda p, lo, hi: d2[i, p, lo:hi], x + 1, ey - 4)
            return c

        def products(x, sums):
            b = density(i, x + 4, 4, 4 + ny)
            a1 = v1[i, x + 3, 3 : 3 + ny]
            a2 = v2[i, x + 2, 2 : 2 + ny]
            dd = d2[i, x + 2, 2 : 2 + ny]
            ww = w[i, x + 1, 1 : 1 + ny]
            r2 = dd - b1 * (g * b - s0 * a1)
            ad1 = g * a1 - s0 * a2
            aw = apply_row(lambda p, lo, hi: w[i, p, lo:hi], x + 1, ey - 6)
            return inner(
                sums,
                ((r2, r2), (r2, ww), (dd, ww), (ww, ww), (r2, ad1), (ww, ad1), (ww, aw)),
            )

        lax.fori_loop(0, ex - 4, row_d, 0)
        lax.fori_loop(0, ex - 6, row_w, 0)
        part[1, i] = pack(lax.fori_loop(0, nx, products, (zero,) * 7))
        return c

    lax.fori_loop(0, nl, second, 0)
    total = all_reduce(1)
    for i in range(nl):
        rr, rw, dw, ww, ra, wa, waw = (unpack(total[i], m) for m in range(7))
        b1 = coef[i, 3]
        s2 = rr / dw
        rr3 = rr - 2.0 * s2 * rw + s2 * s2 * ww
        small = rr3 <= NOISE * rr
        b2 = rr3 / rr
        r_ar = rw - b1 * ra
        w_ar = ww - b1 * wa
        curve = r_ar + s2 * s2 * waw + b2 * b2 * dw
        curve = curve - 2.0 * s2 * w_ar + 2.0 * b2 * rw - 2.0 * s2 * b2 * ww
        s3 = jnp.where(small, 0.0, rr3 / jnp.where(small, 1.0, curve))
        coef[i, 4], coef[i, 5], coef[i, 6] = s2, b2, s3

    weight = weight_ref[...]

    def combine(i):
        s0, g, s1, b1 = coef[i, 0], coef[i, 1], coef[i, 2], coef[i, 3]
        s2, b2, s3 = coef[i, 4], coef[i, 5], coef[i, 6]
        k1 = s1 - s3 * b1
        cb, c1 = s0 + k1 * g, -k1 * s0
        cd, cw = s2 + s3 * (1.0 + b2), -s3 * s2
        cb, c1, cd, cw = cb * weight, c1 * weight, cd * weight, cw * weight

        def row(x, c):
            f = fields_ref[x + 4, 4 : 4 + ny]
            b = f * orb_ref[i, x + 4, 4 : 4 + ny]
            sol = cb * b + c1 * v1[i, x + 3, 3 : 3 + ny]
            sol = sol + cd * d2[i, x + 2, 2 : 2 + ny] + cw * w[i, x + 1, 1 : 1 + ny]
            results[i, x] = -jnp.sum(sol * f, axis=1)
            return c

        lax.fori_loop(0, nx, row, 0)

    def to_band(off):
        target = lax.rem(band + off, n_band)
        return remote(
            results.at[pl.ds(target * per_band, per_band)], results_in.at[off - 1],
            (result_sem.at[0, off - 1], result_sem.at[1, off - 1]), {"band": target},
        )

    def send_results(off, c):
        target = lax.rem(band + off, n_band)
        for k in range(per_band):
            combine(target * per_band + k)
        to_band(off).start()
        return c

    lax.fori_loop(1, n_band, send_results, 0)
    for k in range(per_band):
        combine(band * per_band + k)
    value = results[pl.ds(band * per_band, per_band)]
    for off in range(1, n_band):
        to_band(off).wait()
        value = value + results_in[off - 1]
    out_ref[...] = value


def run(mesh, owner, picked, local, weight):
    n_band, n_gx, n_gy = (mesh.shape[axis] for axis in ("band", "gx", "gy"))
    group = n_gx * n_gy
    turns, n_chip, _, share, nx, ny, nz = picked.shape
    ex, ey, nf = nx + 2 * HALO, ny + 2 * HALO, turns * share
    per_band = local.shape[0]
    nl = per_band * n_band
    vmem = pl.BlockSpec(memory_space=pltpu.VMEM)
    f32 = jnp.float32
    return pl.pallas_call(
        functools.partial(cg_kernel, n_band, n_gx, n_gy),
        out_shape=jax.ShapeDtypeStruct((per_band, nx, ny, nz), f32),
        in_specs=[pl.BlockSpec(memory_space=pltpu.SMEM)] + [vmem] * 3,
        out_specs=vmem,
        scratch_shapes=[
            pltpu.VMEM((ex, ey, nf, nz), f32),
            pltpu.VMEM((nl, ex, ey, 1, nz), f32),
            pltpu.VMEM((turns, n_chip, share, nx, ny, nz), f32),
            pltpu.VMEM((n_chip - 1, turns, share, nx, ny, nz), f32),
            pltpu.VMEM((n_chip - 1, turns, share, nx, ny, nz), f32),
            pltpu.VMEM((nl, nx, ny, nz), f32),
            pltpu.VMEM((n_band - 1, per_band, nx, ny, nz), f32),
            pltpu.VMEM((ex, ey, nf, nz), f32),
            pltpu.VMEM((nl, ex - 2, ey - 2, nf, nz), f32),
            pltpu.VMEM((nl, ex - 4, ey - 4, nf, nz), f32),
            pltpu.VMEM((nl, ex - 4, ey - 4, nf, nz), f32),
            pltpu.VMEM((nl, ex - 6, ey - 6, nf, nz), f32),
            pltpu.VMEM((nl, 7, nf, nz), f32),
            pltpu.VMEM((2, nl, nf, nz), f32),
            pltpu.VMEM((2, group, nl, nf, nz), f32),
            pltpu.SemaphoreType.DMA((2, group)),
            pltpu.SemaphoreType.DMA((2, group)),
            pltpu.SemaphoreType.DMA((2, turns)),
            pltpu.SemaphoreType.DMA((2, n_chip - 1, turns)),
            pltpu.SemaphoreType.DMA((2, n_band)),
            pltpu.SemaphoreType.DMA((2, 2, 4)),
            pltpu.SemaphoreType.DMA((2, n_band - 1)),
        ],
        compiler_params=pltpu.CompilerParams(
            collective_id=0, has_side_effects=True, vmem_limit_bytes=50 << 20
        ),
    )(owner, picked, local, weight)


def on_device(mesh, local_orbitals, block_orbitals, occupation, owner, block_id):
    n_band = mesh.shape["band"]
    band = lax.axis_index("band")
    turns = owner.shape[0]
    blocks_dev, block, nx, ny, nz = block_orbitals.shape
    share = block // n_band
    picked = block_orbitals[block_id]
    picked = picked.reshape(turns, n_band // CORES, CORES, share, nx, ny, nz)
    weights = occupation[owner * blocks_dev + block_id]
    weights = lax.dynamic_slice_in_dim(weights, band * share, share, axis=1)
    weight = jnp.broadcast_to(weights.reshape(-1, 1), (turns * share, nz))
    return run(mesh, owner, picked, local_orbitals[:, :, :, None, :], weight)


def solution(mesh):
    placed = (P("band", "gx", "gy", None), P("band", None, "gx", "gy", None), P(), P(), P())
    return jax.shard_map(
        functools.partial(on_device, mesh),
        mesh=mesh,
        in_specs=placed,
        out_specs=P("band", "gx", "gy", None),
        check_vma=False,
    )
```

```python
import functools

import jax
import jax.numpy as jnp
from jax import lax
from jax.experimental import pallas as pl
from jax.experimental.pallas import tpu as pltpu
from jax.sharding import PartitionSpec as P

SCREEN = 0.1
DIAGONAL = 6.0 + SCREEN
HALO = 4
CORES = 2
SUMS = 8
NOISE = 1e-6


def apply_row(read, x, ny):
    centre = read(x, 1, ny - 1)
    beside = read(x - 1, 1, ny - 1) + read(x + 1, 1, ny - 1)
    beside = beside + read(x, 0, ny - 2) + read(x, 2, ny)
    lanes = centre.shape[-1]
    beside = beside + pltpu.roll(centre, 1, 2) + pltpu.roll(centre, lanes - 1, 2)
    return DIAGONAL * centre - beside


def cg_kernel(
    n_band, n_gx, n_gy, owner_ref, picked_ref, local_ref, weight_ref, out_ref,
    fields_ref, orb_ref, orb_raw, from_mate, combined, from_far, results, results_in,
    dens, v1, v2, d2, w, coef, part, parts, send_sem, recv_sem,
    mate_sem, far_sem, orb_sem, halo_sem, result_sem,
):
    ex, ey, nf, nz = fields_ref.shape
    nl = orb_ref.shape[2]
    turns, n_chip, cores, share = picked_ref.shape[:4]
    per_band = nl // n_band
    nx, ny = ex - 2 * HALO, ey - 2 * HALO
    group = n_gx * n_gy
    band, gx, gy = (lax.axis_index(axis) for axis in ("band", "gx", "gy"))
    me = gx * n_gy + gy
    chip, core = band // cores, lax.rem(band, cores)
    mate = chip * cores + 1 - core
    lane = lax.broadcasted_iota(jnp.int32, (nf, nz), 1)
    inside_x, inside_y = pl.ds(HALO, nx), pl.ds(HALO, ny)

    def device(index):
        return {"gx": index // n_gy, "gy": lax.rem(index, n_gy)}

    def remote(src, dst, sems, target):
        return pltpu.make_async_remote_copy(
            src_ref=src, dst_ref=dst, send_sem=sems[0], recv_sem=sems[1],
            device_id=target, device_id_type=pl.DeviceIdType.MESH,
        )

    barrier = pltpu.get_barrier_semaphore()

    def greet(off, c):
        pl.semaphore_signal(
            barrier, inc=1, device_id=device(lax.rem(me + off, group)),
            device_id_type=pl.DeviceIdType.MESH,
        )
        return c

    def greet_band(off, c):
        pl.semaphore_signal(
            barrier, inc=1, device_id={"band": lax.rem(band + off, n_band)},
            device_id_type=pl.DeviceIdType.MESH,
        )
        return c

    lax.fori_loop(1, group, greet, 0)
    lax.fori_loop(1, n_band, greet_band, 0)
    pl.semaphore_wait(barrier, group + n_band - 2)

    to_mate = [
        remote(
            picked_ref.at[t, :, 1 - core], from_mate.at[t],
            (mate_sem.at[0, t], mate_sem.at[1, t]), {"band": mate},
        )
        for t in range(turns)
    ]
    for copy in to_mate:
        copy.start()
    orb_copies = [
        remote(
            local_ref, orb_raw.at[pl.ds(band * per_band, per_band)],
            (orb_sem.at[0, off], orb_sem.at[1, off]), {"band": lax.rem(band + off, n_band)},
        )
        for off in range(1, n_band)
    ]
    for copy in orb_copies:
        copy.start()
    orb_raw[pl.ds(band * per_band, per_band)] = local_ref[...]
    far = []
    for t in range(turns):
        to_mate[t].wait()
        by_mate = owner_ref[t] == mate
        for off in range(1, n_chip):
            there = lax.rem(chip + off, n_chip)
            combined[off - 1, t] = jnp.where(
                by_mate, from_mate[t, there], picked_ref[t, there, core]
            )
            copy = remote(
                combined.at[off - 1, t], from_far.at[off - 1, t],
                (far_sem.at[0, off - 1, t], far_sem.at[1, off - 1, t]),
                {"band": there * cores + core},
            )
            copy.start()
            far.append((t, copy))

    up, down = {"gx": lax.rem(gx + 1, n_gx)}, {"gx": lax.rem(gx + n_gx - 1, n_gx)}
    right, left = {"gy": lax.rem(gy + 1, n_gy)}, {"gy": lax.rem(gy + n_gy - 1, n_gy)}

    def halo(ref, which):
        def copy(src, dst, target, k):
            sems = (halo_sem.at[0, which, k], halo_sem.at[1, which, k])
            return remote(ref.at[src], ref.at[dst], sems, target)

        def along_y(rows, k):
            return [
                copy((rows, pl.ds(ny, HALO)), (rows, pl.ds(0, HALO)), right, k),
                copy((rows, pl.ds(HALO, HALO)), (rows, pl.ds(HALO + ny, HALO)), left, k + 1),
            ]

        along_x = [
            copy((pl.ds(nx, HALO), inside_y), (pl.ds(0, HALO), inside_y), up, 0),
            copy((pl.ds(HALO, HALO), inside_y), (pl.ds(HALO + nx, HALO), inside_y), down, 1),
        ]
        corners = [along_y(pl.ds(0, HALO), 4), along_y(pl.ds(HALO + nx, HALO), 6)]
        return along_x, along_y(inside_x, 2), corners

    def start_halo(copies):
        for copy in copies[0] + copies[1]:
            copy.start()

    def turn_corners(copies):
        for copy, corners in zip(copies[0], copies[2]):
            copy.wait()
            for corner in corners:
                corner.start()

    def finish_halo(copies):
        for copy in copies[1] + copies[2][0] + copies[2][1]:
            copy.wait()

    for copy in orb_copies:
        copy.wait()
    for i in range(nl):
        orb_ref[inside_x, inside_y, i, :] = orb_raw[i]
    orb_halo, field_halo = halo(orb_ref, 0), halo(fields_ref, 1)
    start_halo(orb_halo)
    for t in range(turns):
        for turn, copy in far:
            if turn == t:
                copy.wait()
        who = owner_ref[t]
        value = jnp.where(who == mate, from_mate[t, chip], picked_ref[t, chip, core])
        for off in range(1, n_chip):
            there = lax.rem(chip + n_chip - off, n_chip)
            value = jnp.where(who // cores == there, from_far[off - 1, t], value)
        for s in range(share):
            fields_ref[inside_x, inside_y, t * share + s, :] = value[s]
    turn_corners(orb_halo)
    start_halo(field_halo)
    turn_corners(field_halo)
    finish_halo(orb_halo)
    finish_halo(field_halo)

    def row0(x, c):
        f = fields_ref[x]
        for i in range(nl):
            dens[i, x] = f * orb_ref[x, :, i : i + 1, :]
        return c

    lax.fori_loop(0, ex, row0, 0)

    def pack(r, i, sums):
        total = part[r]
        for m, acc in enumerate(sums):
            value = jnp.sum(acc, axis=1, keepdims=True)
            total = jnp.where(lane == i * SUMS + m, jnp.broadcast_to(value, (nf, nz)), total)
        part[r] = total

    def unpack(total, i, m):
        value = jnp.sum(jnp.where(lane == i * SUMS + m, total, 0.0), axis=1, keepdims=True)
        return jnp.broadcast_to(value, (nf, nz))

    def copy_to(r, index):
        return pltpu.make_async_remote_copy(
            src_ref=part.at[r], dst_ref=parts.at[r, me],
            send_sem=send_sem.at[r, index], recv_sem=recv_sem.at[r, me],
            device_id=device(index), device_id_type=pl.DeviceIdType.MESH,
        )

    def arrival(r, index):
        return pltpu.make_async_remote_copy(
            src_ref=part.at[r], dst_ref=parts.at[r, index],
            send_sem=send_sem.at[r, index], recv_sem=recv_sem.at[r, index],
            device_id=device(index), device_id_type=pl.DeviceIdType.MESH,
        )

    def all_reduce(r):
        def start(off, c):
            copy_to(r, lax.rem(me + off, group)).start()
            return c

        def finish(off, c):
            index = lax.rem(me + off, group)
            arrival(r, index).wait_recv()
            copy_to(r, index).wait_send()
            return c

        lax.fori_loop(1, group, start, 0)
        parts[r, me] = part[r]
        lax.fori_loop(1, group, finish, 0)
        return lax.fori_loop(1, group, lambda s, t: t + parts[r, s], parts[r, 0])

    def inner(sums, pairs):
        return tuple(s + jnp.sum(a * b, axis=0) for s, (a, b) in zip(sums, pairs))

    zero = jnp.zeros((nf, nz), jnp.float32)
    part[0] = zero
    part[1] = zero

    def basis(i, c):
        def row1(x, c):
            v1[i, x] = apply_row(lambda p, lo, hi: dens[i, p, lo:hi], x + 1, ey)
            return c

        def row2(x, c):
            v2[i, x] = apply_row(lambda p, lo, hi: v1[i, p, lo:hi], x + 1, ey - 2)
            return c

        def products(x, sums):
            b = dens[i, x + 4, 4 : 4 + ny]
            a1 = v1[i, x + 3, 3 : 3 + ny]
            a2 = v2[i, x + 2, 2 : 2 + ny]
            return inner(sums, ((b, b), (b, a1), (a1, a1), (a1, a2), (a2, a2)))

        lax.fori_loop(0, ex - 2, row1, 0)
        lax.fori_loop(0, ex - 4, row2, 0)
        pack(0, i, lax.fori_loop(0, nx, products, (zero,) * 5))
        return c

    lax.fori_loop(0, nl, basis, 0)
    total = all_reduce(0)
    for i in range(nl):
        m0, m1, m2, m3, m4 = (unpack(total, i, m) for m in range(5))
        s0 = m0 / m1
        rr1 = s0 * s0 * m2 - 2.0 * s0 * m1 + m0
        small = rr1 <= NOISE * m0
        b0 = rr1 / m0
        g = 1.0 + b0
        curve = g * g * m1 - 2.0 * g * s0 * m2 + s0 * s0 * m3
        s1 = jnp.where(small, 0.0, rr1 / jnp.where(small, 1.0, curve))
        image2 = g * g * m2 - 2.0 * g * s0 * m3 + s0 * s0 * m4
        rr2 = jnp.maximum(s1 * s1 * image2 - rr1, 0.0)
        b1 = jnp.where(small, 0.0, rr2 / jnp.where(small, 1.0, rr1))
        coef[i, 0], coef[i, 1], coef[i, 2], coef[i, 3] = s0, g, s1, b1

    def second(i, c):
        s0, g, s1, b1 = coef[i, 0], coef[i, 1], coef[i, 2], coef[i, 3]
        cb = 1.0 + b1 * g
        c1 = -(s0 + s1 * g) - b1 * s0
        c2 = s1 * s0

        def row_d(x, c):
            b = dens[i, x + 2, 2 : ey - 2]
            d2[i, x] = cb * b + c1 * v1[i, x + 1, 1 : ey - 3] + c2 * v2[i, x]
            return c

        def row_w(x, c):
            w[i, x] = apply_row(lambda p, lo, hi: d2[i, p, lo:hi], x + 1, ey - 4)
            return c

        def products(x, sums):
            b = dens[i, x + 4, 4 : 4 + ny]
            a1 = v1[i, x + 3, 3 : 3 + ny]
            a2 = v2[i, x + 2, 2 : 2 + ny]
            dd = d2[i, x + 2, 2 : 2 + ny]
            ww = w[i, x + 1, 1 : 1 + ny]
            r2 = dd - b1 * (g * b - s0 * a1)
            ad1 = g * a1 - s0 * a2
            aw = apply_row(lambda p, lo, hi: w[i, p, lo:hi], x + 1, ey - 6)
            return inner(
                sums,
                ((r2, r2), (r2, ww), (dd, ww), (ww, ww), (r2, ad1), (ww, ad1), (ww, aw)),
            )

        lax.fori_loop(0, ex - 4, row_d, 0)
        lax.fori_loop(0, ex - 6, row_w, 0)
        pack(1, i, lax.fori_loop(0, nx, products, (zero,) * 7))
        return c

    lax.fori_loop(0, nl, second, 0)
    total = all_reduce(1)
    for i in range(nl):
        rr, rw, dw, ww, ra, wa, waw = (unpack(total, i, m) for m in range(7))
        b1 = coef[i, 3]
        s2 = rr / dw
        rr3 = rr - 2.0 * s2 * rw + s2 * s2 * ww
        small = rr3 <= NOISE * rr
        b2 = rr3 / rr
        r_ar = rw - b1 * ra
        w_ar = ww - b1 * wa
        curve = r_ar + s2 * s2 * waw + b2 * b2 * dw
        curve = curve - 2.0 * s2 * w_ar + 2.0 * b2 * rw - 2.0 * s2 * b2 * ww
        s3 = jnp.where(small, 0.0, rr3 / jnp.where(small, 1.0, curve))
        coef[i, 4], coef[i, 5], coef[i, 6] = s2, b2, s3

    weight = weight_ref[...]

    def combine(i):
        s0, g, s1, b1 = coef[i, 0], coef[i, 1], coef[i, 2], coef[i, 3]
        s2, b2, s3 = coef[i, 4], coef[i, 5], coef[i, 6]
        k1 = s1 - s3 * b1
        cb, c1 = s0 + k1 * g, -k1 * s0
        cd, cw = s2 + s3 * (1.0 + b2), -s3 * s2
        cb, c1, cd, cw = cb * weight, c1 * weight, cd * weight, cw * weight

        def row(x, c):
            f = fields_ref[x + 4, 4 : 4 + ny]
            b = dens[i, x + 4, 4 : 4 + ny]
            sol = cb * b + c1 * v1[i, x + 3, 3 : 3 + ny]
            sol = sol + cd * d2[i, x + 2, 2 : 2 + ny] + cw * w[i, x + 1, 1 : 1 + ny]
            results[i, x] = -jnp.sum(sol * f, axis=1)
            return c

        lax.fori_loop(0, nx, row, 0)

    def to_band(off):
        target = lax.rem(band + off, n_band)
        return remote(
            results.at[pl.ds(target * per_band, per_band)], results_in.at[off - 1],
            (result_sem.at[0, off - 1], result_sem.at[1, off - 1]), {"band": target},
        )

    def send_results(off, c):
        target = lax.rem(band + off, n_band)
        for k in range(per_band):
            combine(target * per_band + k)
        to_band(off).start()
        return c

    lax.fori_loop(1, n_band, send_results, 0)
    for k in range(per_band):
        combine(band * per_band + k)
    value = results[pl.ds(band * per_band, per_band)]
    for off in range(1, n_band):
        to_band(off).wait()
        value = value + results_in[off - 1]
    out_ref[...] = value


def run(mesh, owner, picked, local, weight):
    n_band, n_gx, n_gy = (mesh.shape[axis] for axis in ("band", "gx", "gy"))
    group = n_gx * n_gy
    turns, n_chip, _, share, nx, ny, nz = picked.shape
    ex, ey, nf = nx + 2 * HALO, ny + 2 * HALO, turns * share
    per_band = local.shape[0]
    nl = per_band * n_band
    vmem = pl.BlockSpec(memory_space=pltpu.VMEM)
    f32 = jnp.float32
    return pl.pallas_call(
        functools.partial(cg_kernel, n_band, n_gx, n_gy),
        out_shape=jax.ShapeDtypeStruct((per_band, nx, ny, nz), f32),
        in_specs=[pl.BlockSpec(memory_space=pltpu.SMEM)] + [vmem] * 3,
        out_specs=vmem,
        scratch_shapes=[
            pltpu.VMEM((ex, ey, nf, nz), f32),
            pltpu.VMEM((ex, ey, nl, nz), f32),
            pltpu.VMEM((nl, nx, ny, nz), f32),
            pltpu.VMEM((turns, n_chip, share, nx, ny, nz), f32),
            pltpu.VMEM((n_chip - 1, turns, share, nx, ny, nz), f32),
            pltpu.VMEM((n_chip - 1, turns, share, nx, ny, nz), f32),
            pltpu.VMEM((nl, nx, ny, nz), f32),
            pltpu.VMEM((n_band - 1, per_band, nx, ny, nz), f32),
            pltpu.VMEM((nl, ex, ey, nf, nz), f32),
            pltpu.VMEM((nl, ex - 2, ey - 2, nf, nz), f32),
            pltpu.VMEM((nl, ex - 4, ey - 4, nf, nz), f32),
            pltpu.VMEM((nl, ex - 4, ey - 4, nf, nz), f32),
            pltpu.VMEM((nl, ex - 6, ey - 6, nf, nz), f32),
            pltpu.VMEM((nl, 7, nf, nz), f32),
            pltpu.VMEM((2, nf, nz), f32),
            pltpu.VMEM((2, group, nf, nz), f32),
            pltpu.SemaphoreType.DMA((2, group)),
            pltpu.SemaphoreType.DMA((2, group)),
            pltpu.SemaphoreType.DMA((2, turns)),
            pltpu.SemaphoreType.DMA((2, n_chip - 1, turns)),
            pltpu.SemaphoreType.DMA((2, n_band)),
            pltpu.SemaphoreType.DMA((2, 2, 8)),
            pltpu.SemaphoreType.DMA((2, n_band - 1)),
        ],
        compiler_params=pltpu.CompilerParams(
            collective_id=0, has_side_effects=True, vmem_limit_bytes=50 << 20
        ),
    )(owner, picked, local, weight)


def on_device(mesh, local_orbitals, block_orbitals, occupation, owner, block_id):
    n_band = mesh.shape["band"]
    band = lax.axis_index("band")
    turns = owner.shape[0]
    blocks_dev, block, nx, ny, nz = block_orbitals.shape
    share = block // n_band
    picked = block_orbitals[block_id]
    picked = picked.reshape(turns, n_band // CORES, CORES, share, nx, ny, nz)
    weights = occupation[owner * blocks_dev + block_id]
    weights = lax.dynamic_slice_in_dim(weights, band * share, share, axis=1)
    weight = jnp.broadcast_to(weights.reshape(-1, 1), (turns * share, nz))
    return run(mesh, owner, picked, local_orbitals, weight)


def solution(mesh):
    placed = (P("band", "gx", "gy", None), P("band", None, "gx", "gy", None), P(), P(), P())
    return jax.shard_map(
        functools.partial(on_device, mesh),
        mesh=mesh,
        in_specs=placed,
        out_specs=P("band", "gx", "gy", None),
        check_vma=False,
    )
```

```python
import functools

import jax
import jax.numpy as jnp
from jax import lax
from jax.experimental import pallas as pl
from jax.experimental.pallas import tpu as pltpu
from jax.sharding import PartitionSpec as P

SCREEN = 0.1
DIAGONAL = 6.0 + SCREEN
HALO = 4
CORES = 2
SUMS = 8
NOISE = 1e-6


def apply_row(read, x, ny):
    centre = read(x, 1, ny - 1)
    beside = read(x - 1, 1, ny - 1) + read(x + 1, 1, ny - 1)
    beside = beside + read(x, 0, ny - 2) + read(x, 2, ny)
    lanes = centre.shape[-1]
    beside = beside + pltpu.roll(centre, 1, 2) + pltpu.roll(centre, lanes - 1, 2)
    return DIAGONAL * centre - beside


def cg_kernel(
    n_band, n_gx, n_gy, owner_ref, picked_ref, local_ref, weight_ref, out_ref,
    fields_ref, orb_ref, orb_raw, arrived, beside, from_mate, combined, from_far, results, results_in,
    dens, v1, v2, d2, w, coef, part, parts, send_sem, recv_sem,
    mate_sem, far_sem, orb_sem, halo_sem, result_sem, beside_sem,
):
    ex, ey, nf, nz = fields_ref.shape
    nl = orb_ref.shape[2]
    turns, n_chip, cores, share = picked_ref.shape[:4]
    per_band = nl // n_band
    nx, ny = ex - 2 * HALO, ey - 2 * HALO
    group = n_gx * n_gy
    band, gx, gy = (lax.axis_index(axis) for axis in ("band", "gx", "gy"))
    me = gx * n_gy + gy
    chip, core = band // cores, lax.rem(band, cores)
    mate = chip * cores + 1 - core
    lane = lax.broadcasted_iota(jnp.int32, (nf, nz), 1)
    inside_x, inside_y = pl.ds(HALO, nx), pl.ds(HALO, ny)

    def device(index):
        return {"gx": index // n_gy, "gy": lax.rem(index, n_gy)}

    def remote(src, dst, sems, target):
        return pltpu.make_async_remote_copy(
            src_ref=src, dst_ref=dst, send_sem=sems[0], recv_sem=sems[1],
            device_id=target, device_id_type=pl.DeviceIdType.MESH,
        )

    barrier = pltpu.get_barrier_semaphore()

    def greet(off, c):
        pl.semaphore_signal(
            barrier, inc=1, device_id=device(lax.rem(me + off, group)),
            device_id_type=pl.DeviceIdType.MESH,
        )
        return c

    def greet_band(off, c):
        pl.semaphore_signal(
            barrier, inc=1, device_id={"band": lax.rem(band + off, n_band)},
            device_id_type=pl.DeviceIdType.MESH,
        )
        return c

    lax.fori_loop(1, group, greet, 0)
    lax.fori_loop(1, n_band, greet_band, 0)
    pl.semaphore_wait(barrier, group + n_band - 2)

    to_mate = [
        remote(
            picked_ref.at[t, :, 1 - core], from_mate.at[t],
            (mate_sem.at[0, t], mate_sem.at[1, t]), {"band": mate},
        )
        for t in range(turns)
    ]
    for copy in to_mate:
        copy.start()
    orb_copies = [
        remote(
            local_ref, orb_raw.at[pl.ds(band * per_band, per_band)],
            (orb_sem.at[0, off], orb_sem.at[1, off]), {"band": lax.rem(band + off, n_band)},
        )
        for off in range(1, n_band)
    ]
    for copy in orb_copies:
        copy.start()
    orb_raw[pl.ds(band * per_band, per_band)] = local_ref[...]
    far = []
    for t in range(turns):
        to_mate[t].wait()
        by_mate = owner_ref[t] == mate
        for off in range(1, n_chip):
            there = lax.rem(chip + off, n_chip)
            combined[off - 1, t] = jnp.where(
                by_mate, from_mate[t, there], picked_ref[t, there, core]
            )
            copy = remote(
                combined.at[off - 1, t], from_far.at[off - 1, t],
                (far_sem.at[0, off - 1, t], far_sem.at[1, off - 1, t]),
                {"band": there * cores + core},
            )
            copy.start()
            far.append((t, copy))

    up, down = {"gx": lax.rem(gx + 1, n_gx)}, {"gx": lax.rem(gx + n_gx - 1, n_gx)}
    right, left = {"gy": lax.rem(gy + 1, n_gy)}, {"gy": lax.rem(gy + n_gy - 1, n_gy)}

    def halo(ref, which):
        def copy(src, dst, target, k):
            sems = (halo_sem.at[0, which, k], halo_sem.at[1, which, k])
            return remote(ref.at[src], ref.at[dst], sems, target)

        def along_y(rows, k):
            return [
                copy((rows, pl.ds(ny, HALO)), (rows, pl.ds(0, HALO)), right, k),
                copy((rows, pl.ds(HALO, HALO)), (rows, pl.ds(HALO + ny, HALO)), left, k + 1),
            ]

        along_x = [
            copy((pl.ds(nx, HALO), inside_y), (pl.ds(0, HALO), inside_y), up, 0),
            copy((pl.ds(HALO, HALO), inside_y), (pl.ds(HALO + nx, HALO), inside_y), down, 1),
        ]
        corners = [along_y(pl.ds(0, HALO), 4), along_y(pl.ds(HALO + nx, HALO), 6)]
        return along_x, along_y(inside_x, 2), corners

    def start_halo(copies):
        for copy in copies[0] + copies[1]:
            copy.start()

    def turn_corners(copies):
        for copy, corners in zip(copies[0], copies[2]):
            copy.wait()
            for corner in corners:
                corner.start()

    def finish_halo(copies):
        for copy in copies[1] + copies[2][0] + copies[2][1]:
            copy.wait()

    for copy in orb_copies:
        copy.wait()
    for i in range(nl):
        orb_ref[inside_x, inside_y, i, :] = orb_raw[i]
    orb_halo, field_halo = halo(orb_ref, 0), halo(fields_ref, 1)
    start_halo(orb_halo)
    rows_in = []
    for t in range(turns):
        for turn, copy in far:
            if turn == t:
                copy.wait()
        who = owner_ref[t]
        value = jnp.where(who == mate, from_mate[t, chip], picked_ref[t, chip, core])
        for off in range(1, n_chip):
            there = lax.rem(chip + n_chip - off, n_chip)
            value = jnp.where(who // cores == there, from_far[off - 1, t], value)
        arrived[t] = value
        for k, (first, target) in enumerate(((nx - HALO, up), (0, down))):
            copy = remote(
                arrived.at[t, :, pl.ds(first, HALO)], beside.at[k, t],
                (beside_sem.at[0, k, t], beside_sem.at[1, k, t]), target,
            )
            copy.start()
            rows_in.append((k, t, copy))
        for s in range(share):
            fields_ref[inside_x, inside_y, t * share + s, :] = value[s]
    turn_corners(orb_halo)
    for copy in field_halo[1]:
        copy.start()
    for k, t, copy in rows_in:
        copy.wait()
        for s in range(share):
            rows = pl.ds(k * (HALO + nx), HALO)
            fields_ref[rows, inside_y, t * share + s, :] = beside[k, t, s]
    for corners in field_halo[2]:
        for corner in corners:
            corner.start()
    finish_halo(orb_halo)
    finish_halo(field_halo)

    def row0(x, c):
        f = fields_ref[x]
        for i in range(nl):
            dens[i, x] = f * orb_ref[x, :, i : i + 1, :]
        return c

    lax.fori_loop(0, ex, row0, 0)

    def pack(r, i, sums):
        total = part[r]
        for m, acc in enumerate(sums):
            value = jnp.sum(acc, axis=1, keepdims=True)
            total = jnp.where(lane == i * SUMS + m, jnp.broadcast_to(value, (nf, nz)), total)
        part[r] = total

    def unpack(total, i, m):
        value = jnp.sum(jnp.where(lane == i * SUMS + m, total, 0.0), axis=1, keepdims=True)
        return jnp.broadcast_to(value, (nf, nz))

    def copy_to(r, index):
        return pltpu.make_async_remote_copy(
            src_ref=part.at[r], dst_ref=parts.at[r, me],
            send_sem=send_sem.at[r, index], recv_sem=recv_sem.at[r, me],
            device_id=device(index), device_id_type=pl.DeviceIdType.MESH,
        )

    def arrival(r, index):
        return pltpu.make_async_remote_copy(
            src_ref=part.at[r], dst_ref=parts.at[r, index],
            send_sem=send_sem.at[r, index], recv_sem=recv_sem.at[r, index],
            device_id=device(index), device_id_type=pl.DeviceIdType.MESH,
        )

    def all_reduce(r):
        def start(off, c):
            copy_to(r, lax.rem(me + off, group)).start()
            return c

        def finish(off, c):
            index = lax.rem(me + off, group)
            arrival(r, index).wait_recv()
            copy_to(r, index).wait_send()
            return c

        lax.fori_loop(1, group, start, 0)
        parts[r, me] = part[r]
        lax.fori_loop(1, group, finish, 0)
        return lax.fori_loop(1, group, lambda s, t: t + parts[r, s], parts[r, 0])

    def inner(sums, pairs):
        return tuple(s + jnp.sum(a * b, axis=0) for s, (a, b) in zip(sums, pairs))

    zero = jnp.zeros((nf, nz), jnp.float32)
    part[0] = zero
    part[1] = zero

    def basis(i, c):
        def row1(x, c):
            v1[i, x] = apply_row(lambda p, lo, hi: dens[i, p, lo:hi], x + 1, ey)
            return c

        def row2(x, c):
            v2[i, x] = apply_row(lambda p, lo, hi: v1[i, p, lo:hi], x + 1, ey - 2)
            return c

        def products(x, sums):
            b = dens[i, x + 4, 4 : 4 + ny]
            a1 = v1[i, x + 3, 3 : 3 + ny]
            a2 = v2[i, x + 2, 2 : 2 + ny]
            return inner(sums, ((b, b), (b, a1), (a1, a1), (a1, a2), (a2, a2)))

        lax.fori_loop(0, ex - 2, row1, 0)
        lax.fori_loop(0, ex - 4, row2, 0)
        pack(0, i, lax.fori_loop(0, nx, products, (zero,) * 5))
        return c

    lax.fori_loop(0, nl, basis, 0)
    total = all_reduce(0)
    for i in range(nl):
        m0, m1, m2, m3, m4 = (unpack(total, i, m) for m in range(5))
        s0 = m0 / m1
        rr1 = s0 * s0 * m2 - 2.0 * s0 * m1 + m0
        small = rr1 <= NOISE * m0
        b0 = rr1 / m0
        g = 1.0 + b0
        curve = g * g * m1 - 2.0 * g * s0 * m2 + s0 * s0 * m3
        s1 = jnp.where(small, 0.0, rr1 / jnp.where(small, 1.0, curve))
        image2 = g * g * m2 - 2.0 * g * s0 * m3 + s0 * s0 * m4
        rr2 = jnp.maximum(s1 * s1 * image2 - rr1, 0.0)
        b1 = jnp.where(small, 0.0, rr2 / jnp.where(small, 1.0, rr1))
        coef[i, 0], coef[i, 1], coef[i, 2], coef[i, 3] = s0, g, s1, b1

    def second(i, c):
        s0, g, s1, b1 = coef[i, 0], coef[i, 1], coef[i, 2], coef[i, 3]
        cb = 1.0 + b1 * g
        c1 = -(s0 + s1 * g) - b1 * s0
        c2 = s1 * s0

        def row_d(x, c):
            b = dens[i, x + 2, 2 : ey - 2]
            d2[i, x] = cb * b + c1 * v1[i, x + 1, 1 : ey - 3] + c2 * v2[i, x]
            return c

        def row_w(x, c):
            w[i, x] = apply_row(lambda p, lo, hi: d2[i, p, lo:hi], x + 1, ey - 4)
            return c

        def products(x, sums):
            b = dens[i, x + 4, 4 : 4 + ny]
            a1 = v1[i, x + 3, 3 : 3 + ny]
            a2 = v2[i, x + 2, 2 : 2 + ny]
            dd = d2[i, x + 2, 2 : 2 + ny]
            ww = w[i, x + 1, 1 : 1 + ny]
            r2 = dd - b1 * (g * b - s0 * a1)
            ad1 = g * a1 - s0 * a2
            aw = apply_row(lambda p, lo, hi: w[i, p, lo:hi], x + 1, ey - 6)
            return inner(
                sums,
                ((r2, r2), (r2, ww), (dd, ww), (ww, ww), (r2, ad1), (ww, ad1), (ww, aw)),
            )

        lax.fori_loop(0, ex - 4, row_d, 0)
        lax.fori_loop(0, ex - 6, row_w, 0)
        pack(1, i, lax.fori_loop(0, nx, products, (zero,) * 7))
        return c

    lax.fori_loop(0, nl, second, 0)
    total = all_reduce(1)
    for i in range(nl):
        rr, rw, dw, ww, ra, wa, waw = (unpack(total, i, m) for m in range(7))
        b1 = coef[i, 3]
        s2 = rr / dw
        rr3 = rr - 2.0 * s2 * rw + s2 * s2 * ww
        small = rr3 <= NOISE * rr
        b2 = rr3 / rr
        r_ar = rw - b1 * ra
        w_ar = ww - b1 * wa
        curve = r_ar + s2 * s2 * waw + b2 * b2 * dw
        curve = curve - 2.0 * s2 * w_ar + 2.0 * b2 * rw - 2.0 * s2 * b2 * ww
        s3 = jnp.where(small, 0.0, rr3 / jnp.where(small, 1.0, curve))
        coef[i, 4], coef[i, 5], coef[i, 6] = s2, b2, s3

    weight = weight_ref[...]

    def combine(i):
        s0, g, s1, b1 = coef[i, 0], coef[i, 1], coef[i, 2], coef[i, 3]
        s2, b2, s3 = coef[i, 4], coef[i, 5], coef[i, 6]
        k1 = s1 - s3 * b1
        cb, c1 = s0 + k1 * g, -k1 * s0
        cd, cw = s2 + s3 * (1.0 + b2), -s3 * s2
        cb, c1, cd, cw = cb * weight, c1 * weight, cd * weight, cw * weight

        def row(x, c):
            f = fields_ref[x + 4, 4 : 4 + ny]
            b = dens[i, x + 4, 4 : 4 + ny]
            sol = cb * b + c1 * v1[i, x + 3, 3 : 3 + ny]
            sol = sol + cd * d2[i, x + 2, 2 : 2 + ny] + cw * w[i, x + 1, 1 : 1 + ny]
            results[i, x] = -jnp.sum(sol * f, axis=1)
            return c

        lax.fori_loop(0, nx, row, 0)

    def to_band(off):
        target = lax.rem(band + off, n_band)
        return remote(
            results.at[pl.ds(target * per_band, per_band)], results_in.at[off - 1],
            (result_sem.at[0, off - 1], result_sem.at[1, off - 1]), {"band": target},
        )

    def send_results(off, c):
        target = lax.rem(band + off, n_band)
        for k in range(per_band):
            combine(target * per_band + k)
        to_band(off).start()
        return c

    lax.fori_loop(1, n_band, send_results, 0)
    for k in range(per_band):
        combine(band * per_band + k)
    value = results[pl.ds(band * per_band, per_band)]
    for off in range(1, n_band):
        to_band(off).wait()
        value = value + results_in[off - 1]
    out_ref[...] = value


def run(mesh, owner, picked, local, weight):
    n_band, n_gx, n_gy = (mesh.shape[axis] for axis in ("band", "gx", "gy"))
    group = n_gx * n_gy
    turns, n_chip, _, share, nx, ny, nz = picked.shape
    ex, ey, nf = nx + 2 * HALO, ny + 2 * HALO, turns * share
    per_band = local.shape[0]
    nl = per_band * n_band
    vmem = pl.BlockSpec(memory_space=pltpu.VMEM)
    f32 = jnp.float32
    return pl.pallas_call(
        functools.partial(cg_kernel, n_band, n_gx, n_gy),
        out_shape=jax.ShapeDtypeStruct((per_band, nx, ny, nz), f32),
        in_specs=[pl.BlockSpec(memory_space=pltpu.SMEM)] + [vmem] * 3,
        out_specs=vmem,
        scratch_shapes=[
            pltpu.VMEM((ex, ey, nf, nz), f32),
            pltpu.VMEM((ex, ey, nl, nz), f32),
            pltpu.VMEM((nl, nx, ny, nz), f32),
            pltpu.VMEM((turns, share, nx, ny, nz), f32),
            pltpu.VMEM((2, turns, share, HALO, ny, nz), f32),
            pltpu.VMEM((turns, n_chip, share, nx, ny, nz), f32),
            pltpu.VMEM((n_chip - 1, turns, share, nx, ny, nz), f32),
            pltpu.VMEM((n_chip - 1, turns, share, nx, ny, nz), f32),
            pltpu.VMEM((nl, nx, ny, nz), f32),
            pltpu.VMEM((n_band - 1, per_band, nx, ny, nz), f32),
            pltpu.VMEM((nl, ex, ey, nf, nz), f32),
            pltpu.VMEM((nl, ex - 2, ey - 2, nf, nz), f32),
            pltpu.VMEM((nl, ex - 4, ey - 4, nf, nz), f32),
            pltpu.VMEM((nl, ex - 4, ey - 4, nf, nz), f32),
            pltpu.VMEM((nl, ex - 6, ey - 6, nf, nz), f32),
            pltpu.VMEM((nl, 7, nf, nz), f32),
            pltpu.VMEM((2, nf, nz), f32),
            pltpu.VMEM((2, group, nf, nz), f32),
            pltpu.SemaphoreType.DMA((2, group)),
            pltpu.SemaphoreType.DMA((2, group)),
            pltpu.SemaphoreType.DMA((2, turns)),
            pltpu.SemaphoreType.DMA((2, n_chip - 1, turns)),
            pltpu.SemaphoreType.DMA((2, n_band)),
            pltpu.SemaphoreType.DMA((2, 2, 8)),
            pltpu.SemaphoreType.DMA((2, n_band - 1)),
            pltpu.SemaphoreType.DMA((2, 2, turns)),
        ],
        compiler_params=pltpu.CompilerParams(
            collective_id=0, has_side_effects=True, vmem_limit_bytes=50 << 20
        ),
    )(owner, picked, local, weight)


def on_device(mesh, local_orbitals, block_orbitals, occupation, owner, block_id):
    n_band = mesh.shape["band"]
    band = lax.axis_index("band")
    turns = owner.shape[0]
    blocks_dev, block, nx, ny, nz = block_orbitals.shape
    share = block // n_band
    picked = block_orbitals[block_id]
    picked = picked.reshape(turns, n_band // CORES, CORES, share, nx, ny, nz)
    weights = occupation[owner * blocks_dev + block_id]
    weights = lax.dynamic_slice_in_dim(weights, band * share, share, axis=1)
    weight = jnp.broadcast_to(weights.reshape(-1, 1), (turns * share, nz))
    return run(mesh, owner, picked, local_orbitals, weight)


def solution(mesh):
    placed = (P("band", "gx", "gy", None), P("band", None, "gx", "gy", None), P(), P(), P())
    return jax.shard_map(
        functools.partial(on_device, mesh),
        mesh=mesh,
        in_specs=placed,
        out_specs=P("band", "gx", "gy", None),
        check_vma=False,
    )
```

```python
import functools

import jax
import jax.numpy as jnp
from jax import lax
from jax.experimental import pallas as pl
from jax.experimental.pallas import tpu as pltpu
from jax.sharding import PartitionSpec as P

SCREEN = 0.1
DIAGONAL = 6.0 + SCREEN
HALO = 4
CORES = 2
SUMS = 8
NOISE = 1e-6


def apply_row(read, x, ny):
    centre = read(x, 1, ny - 1)
    beside = read(x - 1, 1, ny - 1) + read(x + 1, 1, ny - 1)
    beside = beside + read(x, 0, ny - 2) + read(x, 2, ny)
    lanes = centre.shape[-1]
    beside = beside + pltpu.roll(centre, 1, 2) + pltpu.roll(centre, lanes - 1, 2)
    return DIAGONAL * centre - beside


def cg_kernel(
    n_band, n_gx, n_gy, owner_ref, picked_ref, local_ref, weight_ref, out_ref,
    fields_ref, orb_ref, orb_raw, arrived, beside, from_mate, combined, from_far, results, results_in,
    dens, v1, v2, d2, w, coef, part, parts, send_sem, recv_sem,
    mate_sem, far_sem, orb_sem, halo_sem, result_sem, beside_sem,
):
    ex, ey, nf, nz = fields_ref.shape
    nl = orb_ref.shape[2]
    turns, n_chip, cores, share = picked_ref.shape[:4]
    per_band = nl // n_band
    nx, ny = ex - 2 * HALO, ey - 2 * HALO
    group = n_gx * n_gy
    band, gx, gy = (lax.axis_index(axis) for axis in ("band", "gx", "gy"))
    me = gx * n_gy + gy
    chip, core = band // cores, lax.rem(band, cores)
    mate = chip * cores + 1 - core
    lane = lax.broadcasted_iota(jnp.int32, (nf, nz), 1)
    inside_x, inside_y = pl.ds(HALO, nx), pl.ds(HALO, ny)

    def device(index):
        return {"gx": index // n_gy, "gy": lax.rem(index, n_gy)}

    def remote(src, dst, sems, target):
        return pltpu.make_async_remote_copy(
            src_ref=src, dst_ref=dst, send_sem=sems[0], recv_sem=sems[1],
            device_id=target, device_id_type=pl.DeviceIdType.MESH,
        )

    barrier = pltpu.get_barrier_semaphore()

    def greet(off, c):
        pl.semaphore_signal(
            barrier, inc=1, device_id=device(lax.rem(me + off, group)),
            device_id_type=pl.DeviceIdType.MESH,
        )
        return c

    def greet_band(off, c):
        pl.semaphore_signal(
            barrier, inc=1, device_id={"band": lax.rem(band + off, n_band)},
            device_id_type=pl.DeviceIdType.MESH,
        )
        return c

    lax.fori_loop(1, group, greet, 0)
    lax.fori_loop(1, n_band, greet_band, 0)
    pl.semaphore_wait(barrier, group + n_band - 2)

    to_mate = [
        remote(
            picked_ref.at[t, :, 1 - core], from_mate.at[t],
            (mate_sem.at[0, t], mate_sem.at[1, t]), {"band": mate},
        )
        for t in range(turns)
    ]
    for copy in to_mate:
        copy.start()
    orb_copies = [
        remote(
            local_ref, orb_raw.at[pl.ds(band * per_band, per_band)],
            (orb_sem.at[0, off], orb_sem.at[1, off]), {"band": lax.rem(band + off, n_band)},
        )
        for off in range(1, n_band)
    ]
    for copy in orb_copies:
        copy.start()
    orb_raw[pl.ds(band * per_band, per_band)] = local_ref[...]
    far = []
    for t in range(turns):
        to_mate[t].wait()
        by_mate = owner_ref[t] == mate
        for off in range(1, n_chip):
            there = lax.rem(chip + off, n_chip)
            combined[off - 1, t] = jnp.where(
                by_mate, from_mate[t, there], picked_ref[t, there, core]
            )
            copy = remote(
                combined.at[off - 1, t], from_far.at[off - 1, t],
                (far_sem.at[0, off - 1, t], far_sem.at[1, off - 1, t]),
                {"band": there * cores + core},
            )
            copy.start()
            far.append((t, copy))

    up, down = {"gx": lax.rem(gx + 1, n_gx)}, {"gx": lax.rem(gx + n_gx - 1, n_gx)}
    right, left = {"gy": lax.rem(gy + 1, n_gy)}, {"gy": lax.rem(gy + n_gy - 1, n_gy)}

    def halo(ref, which):
        def copy(src, dst, target, k):
            sems = (halo_sem.at[0, which, k], halo_sem.at[1, which, k])
            return remote(ref.at[src], ref.at[dst], sems, target)

        def along_y(rows, k):
            return [
                copy((rows, pl.ds(ny, HALO)), (rows, pl.ds(0, HALO)), right, k),
                copy((rows, pl.ds(HALO, HALO)), (rows, pl.ds(HALO + ny, HALO)), left, k + 1),
            ]

        along_x = [
            copy((pl.ds(nx, HALO), inside_y), (pl.ds(0, HALO), inside_y), up, 0),
            copy((pl.ds(HALO, HALO), inside_y), (pl.ds(HALO + nx, HALO), inside_y), down, 1),
        ]
        corners = [along_y(pl.ds(0, HALO), 4), along_y(pl.ds(HALO + nx, HALO), 6)]
        return along_x, along_y(inside_x, 2), corners

    def start_halo(copies):
        for copy in copies[0] + copies[1]:
            copy.start()

    def turn_corners(copies):
        for copy, corners in zip(copies[0], copies[2]):
            copy.wait()
            for corner in corners:
                corner.start()

    def finish_halo(copies):
        for copy in copies[1] + copies[2][0] + copies[2][1]:
            copy.wait()

    for copy in orb_copies:
        copy.wait()
    for i in range(nl):
        orb_ref[inside_x, inside_y, i, :] = orb_raw[i]
    orb_halo, field_halo = halo(orb_ref, 0), halo(fields_ref, 1)
    start_halo(orb_halo)
    rows_in = []
    for t in range(turns):
        for turn, copy in far:
            if turn == t:
                copy.wait()
        who = owner_ref[t]
        value = jnp.where(who == mate, from_mate[t, chip], picked_ref[t, chip, core])
        for off in range(1, n_chip):
            there = lax.rem(chip + n_chip - off, n_chip)
            value = jnp.where(who // cores == there, from_far[off - 1, t], value)
        arrived[t] = value
        for k, (first, target) in enumerate(((nx - HALO, up), (0, down))):
            copy = remote(
                arrived.at[t, :, pl.ds(first, HALO)], beside.at[k, t],
                (beside_sem.at[0, k, t], beside_sem.at[1, k, t]), target,
            )
            copy.start()
            rows_in.append((k, t, copy))
        for s in range(share):
            fields_ref[inside_x, inside_y, t * share + s, :] = value[s]
    turn_corners(orb_halo)
    for copy in field_halo[1]:
        copy.start()
    for k, t, copy in rows_in:
        copy.wait()
        for s in range(share):
            rows = pl.ds(k * (HALO + nx), HALO)
            fields_ref[rows, inside_y, t * share + s, :] = beside[k, t, s]
    for corners in field_halo[2]:
        for corner in corners:
            corner.start()
    finish_halo(orb_halo)
    finish_halo(field_halo)

    def row0(x, c):
        f = fields_ref[x]
        for i in range(nl):
            dens[i, x] = f * orb_ref[x, :, i : i + 1, :]
        return c

    lax.fori_loop(0, ex, row0, 0)

    def pack(r, i, sums):
        total = part[r]
        for m, acc in enumerate(sums):
            value = jnp.sum(acc, axis=1, keepdims=True)
            total = jnp.where(lane == i * SUMS + m, jnp.broadcast_to(value, (nf, nz)), total)
        part[r] = total

    def unpack(total, i, m):
        value = jnp.sum(jnp.where(lane == i * SUMS + m, total, 0.0), axis=1, keepdims=True)
        return jnp.broadcast_to(value, (nf, nz))

    def copy_to(r, index):
        return pltpu.make_async_remote_copy(
            src_ref=part.at[r], dst_ref=parts.at[r, me],
            send_sem=send_sem.at[r, index], recv_sem=recv_sem.at[r, me],
            device_id=device(index), device_id_type=pl.DeviceIdType.MESH,
        )

    def arrival(r, index):
        return pltpu.make_async_remote_copy(
            src_ref=part.at[r], dst_ref=parts.at[r, index],
            send_sem=send_sem.at[r, index], recv_sem=recv_sem.at[r, index],
            device_id=device(index), device_id_type=pl.DeviceIdType.MESH,
        )

    def all_reduce(r):
        def start(off, c):
            copy_to(r, lax.rem(me + off, group)).start()
            return c

        def finish(off, c):
            index = lax.rem(me + off, group)
            arrival(r, index).wait_recv()
            copy_to(r, index).wait_send()
            return c

        lax.fori_loop(1, group, start, 0)
        parts[r, me] = part[r]
        lax.fori_loop(1, group, finish, 0)
        return lax.fori_loop(1, group, lambda s, t: t + parts[r, s], parts[r, 0])

    def inner(sums, pairs):
        return tuple(s + jnp.sum(a * b, axis=0) for s, (a, b) in zip(sums, pairs))

    zero = jnp.zeros((nf, nz), jnp.float32)
    part[0] = zero
    part[1] = zero

    def basis(i, c):
        def row1(x, c):
            v1[i, x] = apply_row(lambda p, lo, hi: dens[i, p, lo:hi], x + 1, ey)
            return c

        def row2(x, c):
            v2[i, x] = apply_row(lambda p, lo, hi: v1[i, p, lo:hi], x + 1, ey - 2)
            return c

        def products(x, sums):
            b = dens[i, x + 4, 4 : 4 + ny]
            a1 = v1[i, x + 3, 3 : 3 + ny]
            a2 = v2[i, x + 2, 2 : 2 + ny]
            return inner(sums, ((b, b), (b, a1), (a1, a1), (a1, a2), (a2, a2)))

        lax.fori_loop(0, ex - 2, row1, 0)
        lax.fori_loop(0, ex - 4, row2, 0)
        pack(0, i, lax.fori_loop(0, nx, products, (zero,) * 5))
        return c

    lax.fori_loop(0, nl, basis, 0)
    total = all_reduce(0)
    for i in range(nl):
        m0, m1, m2, m3, m4 = (unpack(total, i, m) for m in range(5))
        s0 = m0 / m1
        rr1 = s0 * s0 * m2 - 2.0 * s0 * m1 + m0
        small = rr1 <= NOISE * m0
        b0 = rr1 / m0
        g = 1.0 + b0
        curve = g * g * m1 - 2.0 * g * s0 * m2 + s0 * s0 * m3
        s1 = jnp.where(small, 0.0, rr1 / jnp.where(small, 1.0, curve))
        image2 = g * g * m2 - 2.0 * g * s0 * m3 + s0 * s0 * m4
        rr2 = jnp.maximum(s1 * s1 * image2 - rr1, 0.0)
        b1 = jnp.where(small, 0.0, rr2 / jnp.where(small, 1.0, rr1))
        coef[i, 0], coef[i, 1], coef[i, 2], coef[i, 3] = s0, g, s1, b1

    def second(i, c):
        s0, g, s1, b1 = coef[i, 0], coef[i, 1], coef[i, 2], coef[i, 3]
        cb = 1.0 + b1 * g
        c1 = -(s0 + s1 * g) - b1 * s0
        c2 = s1 * s0

        def row_d(x, c):
            b = dens[i, x + 2, 2 : ey - 2]
            d2[i, x] = cb * b + c1 * v1[i, x + 1, 1 : ey - 3] + c2 * v2[i, x]
            return c

        def row_w(x, c):
            w[i, x] = apply_row(lambda p, lo, hi: d2[i, p, lo:hi], x + 1, ey - 4)
            return c

        def products(x, sums):
            b = dens[i, x + 4, 4 : 4 + ny]
            a1 = v1[i, x + 3, 3 : 3 + ny]
            a2 = v2[i, x + 2, 2 : 2 + ny]
            dd = d2[i, x + 2, 2 : 2 + ny]
            ww = w[i, x + 1, 1 : 1 + ny]
            r2 = dd - b1 * (g * b - s0 * a1)
            ad1 = g * a1 - s0 * a2
            aw = apply_row(lambda p, lo, hi: w[i, p, lo:hi], x + 1, ey - 6)
            return inner(
                sums,
                ((r2, r2), (r2, ww), (dd, ww), (ww, ww), (r2, ad1), (ww, ad1), (ww, aw)),
            )

        lax.fori_loop(0, ex - 4, row_d, 0)
        lax.fori_loop(0, ex - 6, row_w, 0)
        pack(1, i, lax.fori_loop(0, nx, products, (zero,) * 7))
        return c

    lax.fori_loop(0, nl, second, 0)
    total = all_reduce(1)
    for i in range(nl):
        rr, rw, dw, ww, ra, wa, waw = (unpack(total, i, m) for m in range(7))
        b1 = coef[i, 3]
        s2 = rr / dw
        rr3 = rr - 2.0 * s2 * rw + s2 * s2 * ww
        small = rr3 <= NOISE * rr
        b2 = rr3 / rr
        r_ar = rw - b1 * ra
        w_ar = ww - b1 * wa
        curve = r_ar + s2 * s2 * waw + b2 * b2 * dw
        curve = curve - 2.0 * s2 * w_ar + 2.0 * b2 * rw - 2.0 * s2 * b2 * ww
        s3 = jnp.where(small, 0.0, rr3 / jnp.where(small, 1.0, curve))
        coef[i, 4], coef[i, 5], coef[i, 6] = s2, b2, s3

    weight = weight_ref[...]

    def combine(i):
        s0, g, s1, b1 = coef[i, 0], coef[i, 1], coef[i, 2], coef[i, 3]
        s2, b2, s3 = coef[i, 4], coef[i, 5], coef[i, 6]
        k1 = s1 - s3 * b1
        cb, c1 = s0 + k1 * g, -k1 * s0
        cd, cw = s2 + s3 * (1.0 + b2), -s3 * s2
        cb, c1, cd, cw = cb * weight, c1 * weight, cd * weight, cw * weight

        def row(x, c):
            f = fields_ref[x + 4, 4 : 4 + ny]
            b = dens[i, x + 4, 4 : 4 + ny]
            sol = cb * b + c1 * v1[i, x + 3, 3 : 3 + ny]
            sol = sol + cd * d2[i, x + 2, 2 : 2 + ny] + cw * w[i, x + 1, 1 : 1 + ny]
            results[i, x] = -jnp.sum(sol * f, axis=1)
            return c

        lax.fori_loop(0, nx, row, 0)

    def to_band(off):
        target = lax.rem(band + off, n_band)
        return remote(
            results.at[pl.ds(target * per_band, per_band)], results_in.at[off - 1],
            (result_sem.at[0, off - 1], result_sem.at[1, off - 1]), {"band": target},
        )

    def send_results(off, c):
        target = lax.rem(band + off, n_band)
        for k in range(per_band):
            combine(target * per_band + k)
        to_band(off).start()
        return c

    lax.fori_loop(1, n_band, send_results, 0)
    for k in range(per_band):
        combine(band * per_band + k)
    value = results[pl.ds(band * per_band, per_band)]
    for off in range(1, n_band):
        to_band(off).wait()
        value = value + results_in[off - 1]
    out_ref[...] = value


def run(mesh, owner, picked, local, weight):
    n_band, n_gx, n_gy = (mesh.shape[axis] for axis in ("band", "gx", "gy"))
    group = n_gx * n_gy
    turns, n_chip, _, share, nx, ny, nz = picked.shape
    ex, ey, nf = nx + 2 * HALO, ny + 2 * HALO, turns * share
    per_band = local.shape[0]
    nl = per_band * n_band
    vmem = pl.BlockSpec(memory_space=pltpu.VMEM)
    f32 = jnp.float32
    return pl.pallas_call(
        functools.partial(cg_kernel, n_band, n_gx, n_gy),
        out_shape=jax.ShapeDtypeStruct((per_band, nx, ny, nz), f32),
        in_specs=[pl.BlockSpec(memory_space=pltpu.SMEM)] + [vmem] * 3,
        out_specs=vmem,
        scratch_shapes=[
            pltpu.VMEM((ex, ey, nf, nz), f32),
            pltpu.VMEM((ex, ey, nl, nz), f32),
            pltpu.VMEM((nl, nx, ny, nz), f32),
            pltpu.VMEM((turns, share, nx, ny, nz), f32),
            pltpu.VMEM((2, turns, share, HALO, ny, nz), f32),
            pltpu.VMEM((turns, n_chip, share, nx, ny, nz), f32),
            pltpu.VMEM((n_chip - 1, turns, share, nx, ny, nz), f32),
            pltpu.VMEM((n_chip - 1, turns, share, nx, ny, nz), f32),
            pltpu.VMEM((nl, nx, ny, nz), f32),
            pltpu.VMEM((n_band - 1, per_band, nx, ny, nz), f32),
            pltpu.VMEM((nl, ex, ey, nf, nz), f32),
            pltpu.VMEM((nl, ex - 2, ey - 2, nf, nz), f32),
            pltpu.VMEM((nl, ex - 4, ey - 4, nf, nz), f32),
            pltpu.VMEM((nl, ex - 4, ey - 4, nf, nz), f32),
            pltpu.VMEM((nl, ex - 6, ey - 6, nf, nz), f32),
            pltpu.VMEM((nl, 7, nf, nz), f32),
            pltpu.VMEM((2, nf, nz), f32),
            pltpu.VMEM((2, group, nf, nz), f32),
            pltpu.SemaphoreType.DMA((2, group)),
            pltpu.SemaphoreType.DMA((2, group)),
            pltpu.SemaphoreType.DMA((2, turns)),
            pltpu.SemaphoreType.DMA((2, n_chip - 1, turns)),
            pltpu.SemaphoreType.DMA((2, n_band)),
            pltpu.SemaphoreType.DMA((2, 2, 8)),
            pltpu.SemaphoreType.DMA((2, n_band - 1)),
            pltpu.SemaphoreType.DMA((2, 2, turns)),
        ],
        compiler_params=pltpu.CompilerParams(
            collective_id=0, has_side_effects=True, vmem_limit_bytes=50 << 20
        ),
    )(owner, picked, local, weight)


def on_device(mesh, local_orbitals, block_orbitals, occupation, owner, block_id):
    n_band = mesh.shape["band"]
    band = lax.axis_index("band")
    turns = owner.shape[0]
    blocks_dev, block, nx, ny, nz = block_orbitals.shape
    share = block // n_band
    picked = block_orbitals.at[block_id].get(mode="promise_in_bounds")
    picked = picked.reshape(turns, n_band // CORES, CORES, share, nx, ny, nz)
    weights = occupation.at[owner * blocks_dev + block_id].get(mode="promise_in_bounds")
    weights = lax.dynamic_slice_in_dim(weights, band * share, share, axis=1)
    weight = jnp.broadcast_to(weights.reshape(-1, 1), (turns * share, nz))
    return run(mesh, owner, picked, local_orbitals, weight)


def solution(mesh):
    placed = (P("band", "gx", "gy", None), P("band", None, "gx", "gy", None), P(), P(), P())
    return jax.shard_map(
        functools.partial(on_device, mesh),
        mesh=mesh,
        in_specs=placed,
        out_specs=P("band", "gx", "gy", None),
        check_vma=False,
    )
```
